32 devices in a mesh: strip: 2 (over y), col: 4 (over z), row: 4 (over x, core).
Axes of the slice: x: 2, y: 2, z: 4, core: 2. Of those that a mesh axis runs over, the one named last changes fastest.
Arguments:
- left_features: bfloat16 [64, 2048, 128], P(('strip', 'row'), 'col'), parts along dimension 0, may hold values from -6 to 6
- right_features: bfloat16 [64, 2048, 128], P(('strip', 'row'), 'col'), parts along dimension 0, may hold values from -6 to 6
- conv_first: bfloat16 [3, 3, 256, 256], replicated, may hold values from -0.125 to 0.125
- conv_second: bfloat16 [3, 3, 256, 256], replicated, may hold values from -0.125 to 0.125
Outputs:
- cost_field: bfloat16 [64, 2048, 256], P(('strip', 'row'), 'col'), parts along dimension 0
The draws below stay inside these ranges and needn't reach their ends.
There are 2 independent parts, one for each index of `strip`. The reference program is written for one: setup_inputs(seed, part) draws one part's arguments, and reference() takes and returns one part's arrays. A program takes and returns all parts, laid end to end along the dimension named above; an argument that names none is the same for every part. Nothing has to cross between parts.
All inputs are finite; a program needn't handle non-finite values.
Results may differ from the reference program's by a relative error of at most 0.0058.
Values may be sent and summed in bfloat16 or wider, within the bound.
A program may use at most 128 MiB of HBM per device.

```python
import jax
import jax.numpy as jnp
from jax import lax

C = 128
DISP = 256
H = 32
W = 2048


def shard_levels(key, dims, pieces, low, high):
    gain = 1.0
    for position, shards_of in pieces:
        steps = jax.random.uniform(jax.random.fold_in(jax.random.fold_in(key, 6), position), (shards_of,), jnp.float32, low / len(pieces), high / len(pieces))
        gain = gain * jnp.repeat(jnp.exp(steps), dims[position] // shards_of).reshape((-1,) + (1,) * (len(dims) - 1 - position))
    return gain


def gaussian(rng, shape, scale, most, split=(), dtype=jnp.bfloat16):
    values = jax.random.normal(rng, shape, jnp.float32) * scale
    if len(split) > 0:
        values = shard_levels(rng, shape, split, -0.22, 0.18) * values
    return jnp.clip(values, min=-most, max=most).astype(dtype)


def setup_inputs(seed: int = 0, part: int = 0) -> dict:
    splits = jax.random.split(jax.random.key(seed), 5)
    part_splits = jax.random.split(jax.random.fold_in(splits[4], part), 5)
    return {
        "left_features": gaussian(part_splits[0], (H, W, C), 1.0, 6.0, ((0, 4), (1, 4))),
        "right_features": gaussian(part_splits[1], (H, W, C), 1.0, 6.0, ((0, 4), (1, 4))),
        "conv_first": gaussian(splits[2], (3, 3, DISP, DISP), (9 * DISP) ** -0.5, 0.125),
        "conv_second": gaussian(splits[3], (3, 3, DISP, DISP), (9 * DISP) ** -0.5, 0.125),
    }


def correlate(left_part, extended, disparities, chan_count):
    row_count, col_count = (left_part.shape[0], left_part.shape[1])
    block_count = col_count // disparities
    left_blocks = left_part.astype(jnp.float32).reshape(row_count, block_count, disparities, chan_count)
    right_blocks = extended.astype(jnp.float32).reshape(row_count, block_count + 1, disparities, chan_count)
    windows = jnp.concatenate((right_blocks[:, :-1], right_blocks[:, 1:]), axis=2)
    scores = jnp.einsum('rjwc,rjvc->rjwv', left_blocks, windows, precision=lax.Precision.HIGHEST)
    scores = scores * (1.0 / jnp.sqrt(jnp.float32(chan_count)))
    flat_scores = scores.reshape(row_count, block_count, disparities * 2 * disparities)
    flat_scores = jnp.pad(flat_scores, ((0, 0), (0, 0), (0, disparities)))
    skewed = flat_scores.reshape(row_count, block_count, disparities, 2 * disparities + 1)
    banded = skewed[..., 1:disparities + 1][..., ::-1]
    return banded.reshape(row_count, col_count, disparities).astype(jnp.bfloat16)

def convolve_same(image, kernel):
    result = lax.conv_general_dilated(image.astype(jnp.float32)[None], kernel.astype(jnp.float32), (1, 1), 'SAME', dimension_numbers=('NHWC', 'HWIO', 'NHWC'), precision=lax.Precision.HIGHEST)
    return result[0]

def reference(left_features, right_features, conv_first, conv_second):
    zero_cols = jnp.zeros((H, DISP, C), jnp.bfloat16)
    extended = jnp.concatenate((zero_cols, right_features), axis=1)

    def one_row(pair):
        return correlate(pair[0][None], pair[1][None], DISP, C)[0]
    volume = lax.map(one_row, (left_features, extended))
    hidden = jax.nn.relu(convolve_same(volume, conv_first)).astype(jnp.bfloat16)
    return jax.nn.relu(convolve_same(hidden, conv_second)).astype(jnp.bfloat16)
```

```python
import functools

import jax
import jax.numpy as jnp
from jax import lax
from jax.experimental import pallas as pl
from jax.experimental.pallas import tpu as pltpu
from jax.sharding import PartitionSpec as P

MESH = pl.DeviceIdType.MESH
F32 = jnp.float32
BF16 = jnp.bfloat16
G = 16
TILE = 112
LANES = 128


def kernel(
    ncol, nrow, left, right, w1_hbm, w2_hbm, out,
    rext, lext, rrev, vol3, hid3, w1, w2, obuf, lsem, osem, ssem, rsem,
):
    rows, width, chans = left.shape
    disp = w1_hbm.shape[0] // 9
    col = lax.axis_index("col")
    row = lax.axis_index("row")
    has_l, has_r = col > 0, col < ncol - 1
    has_u, has_d = row > 0, row < nrow - 1
    to_l, to_r = {"col": col - 1}, {"col": col + 1}
    to_u, to_d = {"row": row - 1}, {"row": row + 1}
    reach = disp + G
    tiles = vol_cols(width) // TILE
    span = rext.shape[1]
    window = TILE_WINDOW(disp)
    hcols = width + G

    rext[:, 0:reach] = jnp.zeros((rows + 4, reach, chans), BF16)
    rext[:, reach + width :] = jnp.zeros((rows + 4, span - reach - width, chans), BF16)
    lext[:, 0:G] = jnp.zeros((rows + 4, G, chans), BF16)
    lext[:, G + width :] = jnp.zeros((rows + 4, lext.shape[1] - G - width, chans), BF16)
    for ref, at in ((rext, reach), (lext, G)):
        ref[0:2, at : at + width] = jnp.zeros((2, width, chans), BF16)
        ref[rows + 2 :, at : at + width] = jnp.zeros((2, width, chans), BF16)

    own = [
        pltpu.make_async_copy(right, rext.at[2 : rows + 2, reach : reach + width], lsem.at[0]),
        pltpu.make_async_copy(left, lext.at[2 : rows + 2, G : G + width], lsem.at[1]),
        pltpu.make_async_copy(w1_hbm, w1, lsem.at[2]),
        pltpu.make_async_copy(w2_hbm, w2, lsem.at[3]),
    ]
    for copy in own:
        copy.start()

    barrier = pltpu.get_barrier_semaphore()
    for has, to in ((has_l, to_l), (has_r, to_r), (has_u, to_u), (has_d, to_d)):
        @pl.when(has)
        def _():
            pl.semaphore_signal(barrier, inc=1, device_id=to, device_id_type=MESH)
    peers = sum(has.astype(jnp.int32) for has in (has_l, has_r, has_u, has_d))
    pl.semaphore_wait(barrier, peers)

    counter = [0]

    def remote(src, dst, to):
        at = counter[0]
        counter[0] += 1
        return pltpu.make_async_remote_copy(
            src_ref=src, dst_ref=dst, send_sem=ssem.at[at], recv_sem=rsem.at[at],
            device_id=to, device_id_type=MESH,
        )

    tail = width - reach
    far = reach + width
    chunks = [(0, 2), (rows - 2, rows)]
    middle = rows // 2
    chunks += [(2, middle), (middle, rows - 2)]
    small_r = [remote(left.at[:, width - G : width], lext.at[2 : rows + 2, 0:G], to_r)]
    parts = [
        remote(right.at[a:b, tail:width], rext.at[2 + a : 2 + b, 0:reach], to_r)
        for a, b in chunks
    ]
    small_l = [
        remote(left.at[:, 0:G], lext.at[2 : rows + 2, G + width : 2 * G + width], to_l),
        remote(right.at[:, 0:G], rext.at[2 : rows + 2, far : far + G], to_l),
    ]
    down = [
        remote(right.at[rows - 2 : rows], rext.at[0:2, reach:far], to_d),
        remote(left.at[rows - 2 : rows], lext.at[0:2, G : G + width], to_d),
    ]
    up = [
        remote(right.at[0:2], rext.at[rows + 2 : rows + 4, reach:far], to_u),
        remote(left.at[0:2], lext.at[rows + 2 : rows + 4, G : G + width], to_u),
    ]

    def edges(source, target, to):
        s, t = slice(source, source + 2), slice(target, target + 2)
        return [
            remote(rext.at[s, 0:reach], rext.at[t, 0:reach], to),
            remote(rext.at[s, far : far + G], rext.at[t, far : far + G], to),
            remote(lext.at[s, 0:G], lext.at[t, 0:G], to),
            remote(lext.at[s, G + width : 2 * G + width], lext.at[t, G + width : 2 * G + width], to),
        ]

    up_edges = edges(2, rows + 2, to_u)
    down_edges = edges(rows, 0, to_d)

    def start(has, copies):
        @pl.when(has)
        def _():
            for copy in copies:
                copy.start()

    def recv(has, copies):
        @pl.when(has)
        def _():
            for copy in copies:
                copy.wait_recv()

    def sent(has, copies):
        @pl.when(has)
        def _():
            for copy in copies:
                copy.wait_send()

    start(has_r, small_r + parts)
    start(has_l, small_l)
    start(has_d, down)
    start(has_u, up)

    block = span // 4
    i = lax.broadcasted_iota(jnp.int32, (block, block), 0)
    j = lax.broadcasted_iota(jnp.int32, (block, block), 1)
    flip = jnp.where(i + j == block - 1, 1.0, 0.0).astype(BF16)
    scale = 1.0 / jnp.sqrt(F32(chans))

    def correlate(first, count):
        @pl.loop(first, first + count)
        def _(r):
            for q in range(4):
                piece = jnp.dot(
                    flip, rext[r, q * block : (q + 1) * block, :], preferred_element_type=F32
                )
                rrev[(3 - q) * block : (4 - q) * block, :] = piece.astype(BF16)
            for t in range(tiles):
                at = span - window - TILE * t
                scores = lax.dot_general(
                    lext[r, TILE * t : TILE * (t + 1), :],
                    rrev[at : at + window, :],
                    (((1,), (1,)), ((), ())),
                    preferred_element_type=F32,
                )
                turned = pltpu.roll(
                    scores, disp + 1, 1, stride=1, stride_axis=0
                )[:, :disp]
                value = (turned * scale).astype(BF16)
                for b in range(3):
                    vol3[r, TILE * t + 2 - b : TILE * (t + 1) + 2 - b, b * disp : (b + 1) * disp] = value

    def first_conv(first, count):
        @pl.loop(first, first + count)
        def _(g):
            x = jnp.concatenate([vol3[g + a, G : G + hcols, :] for a in range(3)], axis=1)
            acc = jnp.dot(x, w1[...], preferred_element_type=F32)
            j = lax.broadcasted_iota(jnp.int32, (hcols, 1), 0)
            at_row = row * rows + g - 1
            at_col = col * width + j - 1
            inside = (at_col >= 0) & (at_col < ncol * width) & (at_row >= 0) & (at_row < nrow * rows)
            value = jnp.where(inside, jnp.maximum(acc, 0.0), 0.0).astype(BF16)
            for b in range(3):
                hid3[g, G - b : G - b + hcols, b * disp : (b + 1) * disp] = value

    def out_copy(h):
        return pltpu.make_async_copy(obuf.at[h], out.at[h], osem.at[h])

    def second_conv(first, count):
        @pl.loop(first, first + count)
        def _(h):
            x = jnp.concatenate([hid3[h + a, G : G + width, :] for a in range(3)], axis=1)
            acc = jnp.dot(x, w2[...], preferred_element_type=F32)
            obuf[h] = jnp.maximum(acc, 0.0).astype(BF16)
            out_copy(h).start()

    own[0].wait()
    own[1].wait()
    recv(has_l, small_r)
    recv(has_r, small_l)
    recv(has_l, [parts[0]])
    start(has_u, up_edges)
    correlate(2, 2)
    recv(has_l, [parts[1]])
    start(has_d, down_edges)
    correlate(rows, 2)
    recv(has_d, up + up_edges)
    correlate(rows + 2, 2)
    recv(has_l, [parts[2]])
    correlate(4, middle - 2)
    own[2].wait()
    own[3].wait()
    recv(has_u, down + down_edges)
    correlate(0, 2)
    first_conv(0, middle)
    second_conv(0, middle - 2)
    recv(has_l, [parts[3]])
    correlate(middle + 2, middle - 2)
    first_conv(middle, rows + 2 - middle)
    second_conv(middle - 2, rows + 2 - middle)

    sent(has_r, small_r + parts)
    sent(has_l, small_l)
    sent(has_d, down + down_edges)
    sent(has_u, up + up_edges)

    @pl.loop(0, rows)
    def _(h):
        out_copy(h).wait()


def vol_cols(width):
    return -(-(width + 2 * G) // TILE) * TILE


def TILE_WINDOW(disp):
    return -(-(TILE + disp - 1) // LANES) * LANES


def local(ncol, nrow, left, right, w1, w2):
    rows, width, chans = left.shape
    disp = w1.shape[2]
    outs = w1.shape[3]
    w1 = w1.reshape(-1, outs)
    w2 = w2.reshape(-1, outs)
    span = vol_cols(width) - TILE + TILE_WINDOW(disp)
    hbm = pl.BlockSpec(memory_space=pl.ANY)
    copies = 19
    return pl.pallas_call(
        functools.partial(fixed, ncol, nrow),
        out_shape=jax.ShapeDtypeStruct((rows, width, outs), BF16),
        in_specs=[hbm] * 4,
        out_specs=hbm,
        scratch_shapes=[
            pltpu.VMEM((rows + 4, span, chans), BF16),
            pltpu.VMEM((rows + 4, vol_cols(width), chans), BF16),
            pltpu.VMEM((span, chans), BF16),
            pltpu.VMEM((rows + 4, vol_cols(width) + G, 3 * disp), BF16),
            pltpu.VMEM((rows + 2, width + 3 * G, 3 * outs), BF16),
            pltpu.VMEM(w1.shape, BF16),
            pltpu.VMEM(w2.shape, BF16),
            pltpu.VMEM((rows, width, outs), BF16),
            pltpu.SemaphoreType.DMA((4,)),
            pltpu.SemaphoreType.DMA((rows,)),
            pltpu.SemaphoreType.DMA((copies,)),
            pltpu.SemaphoreType.DMA((copies,)),
        ],
        compiler_params=pltpu.CompilerParams(
            collective_id=0, has_side_effects=True, vmem_limit_bytes=60 * 1024 * 1024
        ),
    )(left, right, w1, w2)


def fixed(ncol, nrow, *refs):
    kernel(ncol, nrow, *refs)


def solution(mesh):
    in_specs = (P(("strip", "row"), "col", None), P(("strip", "row"), "col", None), P(), P())
    out_specs = P(("strip", "row"), "col", None)
    return jax.shard_map(
        functools.partial(local, mesh.shape["col"], mesh.shape["row"]),
        mesh=mesh, in_specs=in_specs, out_specs=out_specs, check_vma=False,
    )
```

```python
import functools

import jax
import jax.numpy as jnp
from jax import lax
from jax.experimental import pallas as pl
from jax.experimental.pallas import tpu as pltpu
from jax.sharding import PartitionSpec as P

MESH = pl.DeviceIdType.MESH
F32 = jnp.float32
BF16 = jnp.bfloat16
G = 16
TILE = 112
LANES = 128


def kernel(
    ncol, nrow, left, right, w1_hbm, w2_hbm, out,
    rext, lext, rrev, vol3, hid3, w1, w2, lsem, ssem, rsem,
):
    rows, width, chans = left.shape
    disp = w1_hbm.shape[0] // 9
    col = lax.axis_index("col")
    row = lax.axis_index("row")
    has_l, has_r = col > 0, col < ncol - 1
    has_u, has_d = row > 0, row < nrow - 1
    to_l, to_r = {"col": col - 1}, {"col": col + 1}
    to_u, to_d = {"row": row - 1}, {"row": row + 1}
    reach = disp + G
    tiles = vol_cols(width) // TILE
    span = rext.shape[1]
    window = TILE_WINDOW(disp)
    hcols = width + G

    own = [
        pltpu.make_async_copy(right, rext.at[2 : rows + 2, reach : reach + width], lsem.at[0]),
        pltpu.make_async_copy(left, lext.at[2 : rows + 2, G : G + width], lsem.at[1]),
        pltpu.make_async_copy(w1_hbm, w1, lsem.at[2]),
        pltpu.make_async_copy(w2_hbm, w2, lsem.at[3]),
    ]
    for copy in own:
        copy.start()

    edge = reach + width
    rext[:, edge + G :] = jnp.zeros((rows + 4, span - edge - G, chans), BF16)
    lext[:, 2 * G + width :] = jnp.zeros((rows + 4, lext.shape[1] - 2 * G - width, chans), BF16)

    def clear(ref, *at):
        ref[at] = jnp.zeros(ref.at[at].shape, BF16)

    @pl.when(jnp.logical_not(has_l))
    def _():
        clear(rext, slice(0, rows + 4), slice(0, reach))
        clear(lext, slice(0, rows + 4), slice(0, G))

    @pl.when(jnp.logical_not(has_r))
    def _():
        clear(rext, slice(0, rows + 4), slice(edge, edge + G))
        clear(lext, slice(0, rows + 4), slice(G + width, 2 * G + width))

    @pl.when(jnp.logical_not(has_u))
    def _():
        clear(rext, slice(0, 2), slice(0, edge + G))
        clear(lext, slice(0, 2), slice(0, 2 * G + width))

    @pl.when(jnp.logical_not(has_d))
    def _():
        clear(rext, slice(rows + 2, rows + 4), slice(0, edge + G))
        clear(lext, slice(rows + 2, rows + 4), slice(0, 2 * G + width))

    barrier = pltpu.get_barrier_semaphore()
    for has, to in ((has_l, to_l), (has_r, to_r), (has_u, to_u), (has_d, to_d)):
        @pl.when(has)
        def _():
            pl.semaphore_signal(barrier, inc=1, device_id=to, device_id_type=MESH)
    peers = sum(has.astype(jnp.int32) for has in (has_l, has_r, has_u, has_d))
    pl.semaphore_wait(barrier, peers)

    counter = [0]

    def remote(src, dst, to):
        at = counter[0]
        counter[0] += 1
        return pltpu.make_async_remote_copy(
            src_ref=src, dst_ref=dst, send_sem=ssem.at[at], recv_sem=rsem.at[at],
            device_id=to, device_id_type=MESH,
        )

    tail = width - reach
    far = reach + width
    chunks = [(0, 2), (rows - 2, rows)]
    middle = rows // 2
    chunks += [(2, middle), (middle, rows - 2)]
    small_r = [remote(left.at[:, width - G : width], lext.at[2 : rows + 2, 0:G], to_r)]
    parts = [
        remote(right.at[a:b, tail:width], rext.at[2 + a : 2 + b, 0:reach], to_r)
        for a, b in chunks
    ]
    small_l = [
        remote(left.at[:, 0:G], lext.at[2 : rows + 2, G + width : 2 * G + width], to_l),
        remote(right.at[:, 0:G], rext.at[2 : rows + 2, far : far + G], to_l),
    ]
    down = [
        remote(right.at[rows - 2 : rows], rext.at[0:2, reach:far], to_d),
        remote(left.at[rows - 2 : rows], lext.at[0:2, G : G + width], to_d),
    ]
    up = [
        remote(right.at[0:2], rext.at[rows + 2 : rows + 4, reach:far], to_u),
        remote(left.at[0:2], lext.at[rows + 2 : rows + 4, G : G + width], to_u),
    ]

    def edges(source, target, to):
        s, t = slice(source, source + 2), slice(target, target + 2)
        return [
            remote(rext.at[s, 0:reach], rext.at[t, 0:reach], to),
            remote(rext.at[s, far : far + G], rext.at[t, far : far + G], to),
            remote(lext.at[s, 0:G], lext.at[t, 0:G], to),
            remote(lext.at[s, G + width : 2 * G + width], lext.at[t, G + width : 2 * G + width], to),
        ]

    up_edges = edges(2, rows + 2, to_u)
    down_edges = edges(rows, 0, to_d)

    def start(has, copies):
        @pl.when(has)
        def _():
            for copy in copies:
                copy.start()

    def recv(has, copies):
        @pl.when(has)
        def _():
            for copy in copies:
                copy.wait_recv()

    def sent(has, copies):
        @pl.when(has)
        def _():
            for copy in copies:
                copy.wait_send()

    start(has_r, small_r + parts)
    start(has_l, small_l)
    start(has_d, down)
    start(has_u, up)

    scale = 1.0 / jnp.sqrt(F32(chans))
    cut = -(-reach // TILE)
    fresh = -(-(span - TILE * cut) // (2 * G)) * (2 * G)

    def flip(size):
        i = lax.broadcasted_iota(jnp.int32, (size, size), 0)
        j = lax.broadcasted_iota(jnp.int32, (size, size), 1)
        return jnp.where(i + j == size - 1, 1.0, 0.0).astype(BF16)

    def correlate(first, count, right_part):
        size = fresh // 2 if right_part else (span - fresh) // 2
        base = 0 if right_part else fresh

        @pl.loop(0, count // 2)
        def _(p):
            pair = [first + 2 * p, first + 2 * p + 1]
            turn = flip(size)
            for q in range(2):
                for r in pair:
                    high = span - base - q * size
                    piece = jnp.dot(turn, rext[r, high - size : high, :], preferred_element_type=F32)
                    rrev[r, base + q * size : base + (q + 1) * size, :] = piece.astype(BF16)
            for t in range(cut, tiles) if right_part else range(cut):
                at = span - window - TILE * t
                for r in pair:
                    scores = lax.dot_general(
                        lext[r, TILE * t : TILE * (t + 1), :],
                        rrev[r, at : at + window, :],
                        (((1,), (1,)), ((), ())),
                        preferred_element_type=F32,
                    )
                    turned = pltpu.roll(
                        scores, window - TILE_SHIFT(disp), 1, stride=1, stride_axis=0
                    )[:, :disp]
                    value = (turned * scale).astype(BF16)
                    for b in range(3):
                        vol3[r, TILE * t + 2 - b : TILE * (t + 1) + 2 - b, b * disp : (b + 1) * disp] = value

    bar = -(-(TILE * cut + 2) // G) * G

    def first_conv(first, count, right_part):
        low, high = (bar, G + hcols) if right_part else (G, bar)
        size = high - low

        @pl.loop(0, count // 2)
        def _(p):
            g = first + 2 * p
            x = jnp.concatenate(
                [vol3[pl.ds(g + a, 2), low:high, :].reshape(2 * size, 3 * disp) for a in range(3)], axis=1
            )
            acc = jnp.dot(x, w1[...], preferred_element_type=F32)
            j = lax.broadcasted_iota(jnp.int32, (size, 1), 0)
            at_col = col * width + j + (low - G - 1)
            inside_col = (at_col >= 0) & (at_col < ncol * width)
            for k in range(2):
                at_row = row * rows + g + k - 1
                inside = inside_col & (at_row >= 0) & (at_row < nrow * rows)
                value = jnp.maximum(acc[k * size : (k + 1) * size], 0.0)
                value = jnp.where(inside, value, 0.0).astype(BF16)
                for b in range(3):
                    hid3[g + k, low - b : high - b, b * disp : (b + 1) * disp] = value

    def second_conv(first, count, right_part):
        low, high = (bar, G + width) if right_part else (G, bar)
        size = high - low

        @pl.loop(0, count // 2)
        def _(p):
            h = first + 2 * p
            x = jnp.concatenate(
                [hid3[pl.ds(h + a, 2), low:high, :].reshape(2 * size, 3 * disp) for a in range(3)], axis=1
            )
            acc = jnp.dot(x, w2[...], preferred_element_type=F32)
            out[pl.ds(h, 2), low - G : high - G] = jnp.maximum(acc, 0.0).astype(BF16).reshape(2, size, disp)

    RIGHT, LEFT = True, False
    own[0].wait()
    own[1].wait()
    recv(has_r, small_l)
    correlate(2, rows, RIGHT)
    recv(has_l, small_r + [parts[0]])
    start(has_u, up_edges)
    own[2].wait()
    first_conv(2, rows - 2, RIGHT)
    own[3].wait()
    second_conv(2, rows - 4, RIGHT)
    correlate(2, 2, LEFT)
    recv(has_l, [parts[1]])
    start(has_d, down_edges)
    correlate(rows, 2, LEFT)
    recv(has_d, up + up_edges)
    correlate(rows + 2, 2, RIGHT)
    correlate(rows + 2, 2, LEFT)
    first_conv(rows, 2, RIGHT)
    first_conv(rows, 2, LEFT)
    second_conv(rows - 2, 2, RIGHT)
    recv(has_l, [parts[2]])
    correlate(4, middle - 2, LEFT)
    first_conv(2, middle - 2, LEFT)
    recv(has_u, down + down_edges)
    correlate(0, 2, RIGHT)
    correlate(0, 2, LEFT)
    first_conv(0, 2, RIGHT)
    first_conv(0, 2, LEFT)
    second_conv(0, 2, RIGHT)
    second_conv(0, middle - 2, LEFT)
    recv(has_l, [parts[3]])
    correlate(middle + 2, rows - 2 - middle, LEFT)
    first_conv(middle, rows - middle, LEFT)
    second_conv(middle - 2, rows + 2 - middle, LEFT)

    sent(has_r, small_r + parts)
    sent(has_l, small_l)
    sent(has_d, down + down_edges)
    sent(has_u, up + up_edges)


def TILE_SHIFT(disp):
    return TILE_WINDOW(disp) - disp - 1


def vol_cols(width):
    return -(-(width + 2 * G) // TILE) * TILE


def TILE_WINDOW(disp):
    return -(-(TILE + disp - 1) // LANES) * LANES


def local(ncol, nrow, left, right, w1, w2):
    rows, width, chans = left.shape
    disp = w1.shape[2]
    outs = w1.shape[3]
    w1 = w1.reshape(-1, outs)
    w2 = w2.reshape(-1, outs)
    span = vol_cols(width) - TILE + TILE_WINDOW(disp)
    hbm = pl.BlockSpec(memory_space=pl.ANY)
    copies = 19
    return pl.pallas_call(
        functools.partial(fixed, ncol, nrow),
        out_shape=pltpu.VMEM((rows, width, outs), BF16),
        in_specs=[hbm] * 4,
        out_specs=pl.BlockSpec(memory_space=pltpu.VMEM),
        scratch_shapes=[
            pltpu.VMEM((rows + 4, span, chans), BF16),
            pltpu.VMEM((rows + 4, vol_cols(width), chans), BF16),
            pltpu.VMEM((rows + 4, span, chans), BF16),
            pltpu.VMEM((rows + 4, vol_cols(width) + G, 3 * disp), BF16),
            pltpu.VMEM((rows + 2, width + 3 * G, 3 * outs), BF16),
            pltpu.VMEM(w1.shape, BF16),
            pltpu.VMEM(w2.shape, BF16),
            pltpu.SemaphoreType.DMA((4,)),
            pltpu.SemaphoreType.DMA((copies,)),
            pltpu.SemaphoreType.DMA((copies,)),
        ],
        compiler_params=pltpu.CompilerParams(
            collective_id=0, has_side_effects=True, vmem_limit_bytes=67_043_328 - 2 * rows * width * outs - 2**18
        ),
    )(left, right, w1, w2)


def fixed(ncol, nrow, *refs):
    kernel(ncol, nrow, *refs)


def solution(mesh):
    in_specs = (P(("strip", "row"), "col", None), P(("strip", "row"), "col", None), P(), P())
    out_specs = P(("strip", "row"), "col", None)
    return jax.shard_map(
        functools.partial(local, mesh.shape["col"], mesh.shape["row"]),
        mesh=mesh, in_specs=in_specs, out_specs=out_specs, check_vma=False,
    )
```

```python
import functools

import jax
import jax.numpy as jnp
from jax import lax
from jax.experimental import pallas as pl
from jax.experimental.pallas import tpu as pltpu
from jax.sharding import PartitionSpec as P

MESH = pl.DeviceIdType.MESH
F32 = jnp.float32
BF16 = jnp.bfloat16
G = 16
TILE = 112
LANES = 128


def kernel(
    ncol, nrow, left, right, w1_hbm, w2_hbm, out,
    rext, lext, rrev, vol3, hid3, w1, w2, lsem, ssem, rsem,
):
    rows, width, chans = left.shape
    disp = w1_hbm.shape[0] // 9
    col = lax.axis_index("col")
    row = lax.axis_index("row")
    has_l, has_r = col > 0, col < ncol - 1
    has_u, has_d = row > 0, row < nrow - 1
    to_l, to_r = {"col": col - 1}, {"col": col + 1}
    to_u, to_d = {"row": row - 1}, {"row": row + 1}
    reach = disp + G
    tiles = vol_cols(width) // TILE
    span = rext.shape[1]
    window = TILE_WINDOW(disp)
    hcols = width + G

    own = [
        pltpu.make_async_copy(right, rext.at[2 : rows + 2, reach : reach + width], lsem.at[0]),
        pltpu.make_async_copy(left, lext.at[2 : rows + 2, G : G + width], lsem.at[1]),
        pltpu.make_async_copy(w1_hbm, w1, lsem.at[2]),
        pltpu.make_async_copy(w2_hbm, w2, lsem.at[3]),
    ]
    for copy in own:
        copy.start()

    edge = reach + width
    rext[:, edge + G :] = jnp.zeros((rows + 4, span - edge - G, chans), BF16)
    lext[:, 2 * G + width :] = jnp.zeros((rows + 4, lext.shape[1] - 2 * G - width, chans), BF16)

    def clear(ref, *at):
        ref[at] = jnp.zeros(ref.at[at].shape, BF16)

    @pl.when(jnp.logical_not(has_l))
    def _():
        clear(rext, slice(0, rows + 4), slice(0, reach))
        clear(lext, slice(0, rows + 4), slice(0, G))

    @pl.when(jnp.logical_not(has_r))
    def _():
        clear(rext, slice(0, rows + 4), slice(edge, edge + G))
        clear(lext, slice(0, rows + 4), slice(G + width, 2 * G + width))

    @pl.when(jnp.logical_not(has_u))
    def _():
        clear(rext, slice(0, 2), slice(0, edge + G))
        clear(lext, slice(0, 2), slice(0, 2 * G + width))

    @pl.when(jnp.logical_not(has_d))
    def _():
        clear(rext, slice(rows + 2, rows + 4), slice(0, edge + G))
        clear(lext, slice(rows + 2, rows + 4), slice(0, 2 * G + width))

    barrier = pltpu.get_barrier_semaphore()
    for has, to in ((has_l, to_l), (has_r, to_r), (has_u, to_u), (has_d, to_d)):
        @pl.when(has)
        def _():
            pl.semaphore_signal(barrier, inc=1, device_id=to, device_id_type=MESH)
    peers = sum(has.astype(jnp.int32) for has in (has_l, has_r, has_u, has_d))
    pl.semaphore_wait(barrier, peers)

    counter = [0]

    def remote(src, dst, to):
        at = counter[0]
        counter[0] += 1
        return pltpu.make_async_remote_copy(
            src_ref=src, dst_ref=dst, send_sem=ssem.at[at], recv_sem=rsem.at[at],
            device_id=to, device_id_type=MESH,
        )

    tail = width - reach
    far = reach + width
    chunks = [(0, 2), (rows - 2, rows)]
    middle = rows // 2
    chunks += [(2, middle), (middle, rows - 2)]
    small_r = [remote(left.at[:, width - G : width], lext.at[2 : rows + 2, 0:G], to_r)]
    parts = [
        remote(right.at[a:b, tail:width], rext.at[2 + a : 2 + b, 0:reach], to_r)
        for a, b in chunks
    ]
    small_l = [
        remote(left.at[:, 0:G], lext.at[2 : rows + 2, G + width : 2 * G + width], to_l),
        remote(right.at[:, 0:G], rext.at[2 : rows + 2, far : far + G], to_l),
    ]
    down = [
        remote(right.at[rows - 2 : rows], rext.at[0:2, reach:far], to_d),
        remote(left.at[rows - 2 : rows], lext.at[0:2, G : G + width], to_d),
    ]
    up = [
        remote(right.at[0:2], rext.at[rows + 2 : rows + 4, reach:far], to_u),
        remote(left.at[0:2], lext.at[rows + 2 : rows + 4, G : G + width], to_u),
    ]

    def edges(source, target, to):
        s, t = slice(source, source + 2), slice(target, target + 2)
        return [
            remote(rext.at[s, 0:reach], rext.at[t, 0:reach], to),
            remote(rext.at[s, far : far + G], rext.at[t, far : far + G], to),
            remote(lext.at[s, 0:G], lext.at[t, 0:G], to),
            remote(lext.at[s, G + width : 2 * G + width], lext.at[t, G + width : 2 * G + width], to),
        ]

    up_edges = edges(2, rows + 2, to_u)
    down_edges = edges(rows, 0, to_d)

    def start(has, copies):
        @pl.when(has)
        def _():
            for copy in copies:
                copy.start()

    def recv(has, copies):
        @pl.when(has)
        def _():
            for copy in copies:
                copy.wait_recv()

    def sent(has, copies):
        @pl.when(has)
        def _():
            for copy in copies:
                copy.wait_send()

    start(has_r, small_r + parts)
    start(has_l, small_l)
    start(has_d, down)
    start(has_u, up)

    scale = 1.0 / jnp.sqrt(F32(chans))
    cut = -(-reach // TILE)
    fresh = -(-(span - TILE * cut) // (2 * G)) * (2 * G)

    def flip(size):
        i = lax.broadcasted_iota(jnp.int32, (size, size), 0)
        j = lax.broadcasted_iota(jnp.int32, (size, size), 1)
        return jnp.where(i + j == size - 1, 1.0, 0.0).astype(BF16)

    def correlate(first, count, right_part):
        step = 4 if count % 4 == 0 else 2
        size = fresh // 2 if right_part else (span - fresh) // 2
        base = 0 if right_part else fresh

        @pl.loop(0, count // step)
        def _(p):
            pair = [first + step * p + k for k in range(step)]
            turn = flip(size)
            for q in range(2):
                for r in pair:
                    high = span - base - q * size
                    piece = jnp.dot(turn, rext[r, high - size : high, :], preferred_element_type=F32)
                    rrev[r, base + q * size : base + (q + 1) * size, :] = piece.astype(BF16)
            for t in range(cut, tiles) if right_part else range(cut):
                at = span - window - TILE * t
                for r in pair:
                    scores = lax.dot_general(
                        lext[r, TILE * t : TILE * (t + 1), :],
                        rrev[r, at : at + window, :],
                        (((1,), (1,)), ((), ())),
                        preferred_element_type=F32,
                    )
                    turned = pltpu.roll(
                        scores, window - TILE_SHIFT(disp), 1, stride=1, stride_axis=0
                    )[:, :disp]
                    value = (turned * scale).astype(BF16)
                    for b in range(3):
                        vol3[r, TILE * t + 2 - b : TILE * (t + 1) + 2 - b, b * disp : (b + 1) * disp] = value

    bar = -(-(TILE * cut + 2) // G) * G

    def first_conv(first, count, right_part):
        low, high = (bar, G + hcols) if right_part else (G, bar)
        size = high - low

        @pl.loop(0, count // 2)
        def _(p):
            g = first + 2 * p
            x = jnp.concatenate(
                [vol3[pl.ds(g + a, 2), low:high, :].reshape(2 * size, 3 * disp) for a in range(3)], axis=1
            )
            acc = jnp.dot(x, w1[...], preferred_element_type=F32)
            j = lax.broadcasted_iota(jnp.int32, (size, 1), 0)
            at_col = col * width + j + (low - G - 1)
            inside_col = (at_col >= 0) & (at_col < ncol * width)
            for k in range(2):
                at_row = row * rows + g + k - 1
                inside = inside_col & (at_row >= 0) & (at_row < nrow * rows)
                value = jnp.maximum(acc[k * size : (k + 1) * size], 0.0)
                value = jnp.where(inside, value, 0.0).astype(BF16)
                for b in range(3):
                    hid3[g + k, low - b : high - b, b * disp : (b + 1) * disp] = value

    def second_conv(first, count, right_part):
        low, high = (bar, G + width) if right_part else (G, bar)
        size = high - low

        @pl.loop(0, count // 2)
        def _(p):
            h = first + 2 * p
            x = jnp.concatenate(
                [hid3[pl.ds(h + a, 2), low:high, :].reshape(2 * size, 3 * disp) for a in range(3)], axis=1
            )
            acc = jnp.dot(x, w2[...], preferred_element_type=F32)
            out[pl.ds(h, 2), low - G : high - G] = jnp.maximum(acc, 0.0).astype(BF16).reshape(2, size, disp)

    RIGHT, LEFT = True, False
    own[0].wait()
    own[1].wait()
    recv(has_r, small_l)
    start(has_u, up_edges[1::2])
    start(has_d, down_edges[1::2])
    correlate(2, rows, RIGHT)
    own[2].wait()
    first_conv(2, rows - 2, RIGHT)
    recv(has_l, small_r + [parts[0]])
    start(has_u, up_edges[0::2])
    own[3].wait()
    second_conv(2, rows - 4, RIGHT)
    recv(has_d, up + up_edges[1::2])
    correlate(rows + 2, 2, RIGHT)
    recv(has_l, [parts[1]])
    start(has_d, down_edges[0::2])
    recv(has_u, down + down_edges[1::2])
    correlate(0, 2, RIGHT)
    first_conv(rows, 2, RIGHT)
    first_conv(0, 2, RIGHT)
    second_conv(rows - 2, 2, RIGHT)
    second_conv(0, 2, RIGHT)
    correlate(2, 2, LEFT)
    correlate(rows, 2, LEFT)
    recv(has_d, up_edges[0::2])
    correlate(rows + 2, 2, LEFT)
    first_conv(rows, 2, LEFT)
    recv(has_l, [parts[2]])
    correlate(4, middle - 2, LEFT)
    first_conv(2, middle - 2, LEFT)
    recv(has_u, down_edges[0::2])
    correlate(0, 2, LEFT)
    first_conv(0, 2, LEFT)
    second_conv(0, middle - 2, LEFT)
    recv(has_l, [parts[3]])
    correlate(middle + 2, rows - 2 - middle, LEFT)
    first_conv(middle, rows - middle, LEFT)
    second_conv(middle - 2, rows + 2 - middle, LEFT)

    sent(has_r, small_r + parts)
    sent(has_l, small_l)
    sent(has_d, down + down_edges)
    sent(has_u, up + up_edges)


def TILE_SHIFT(disp):
    return TILE_WINDOW(disp) - disp - 1


def vol_cols(width):
    return -(-(width + 2 * G) // TILE) * TILE


def TILE_WINDOW(disp):
    return -(-(TILE + disp - 1) // LANES) * LANES


def local(ncol, nrow, left, right, w1, w2):
    rows, width, chans = left.shape
    disp = w1.shape[2]
    outs = w1.shape[3]
    w1 = w1.reshape(-1, outs)
    w2 = w2.reshape(-1, outs)
    span = vol_cols(width) - TILE + TILE_WINDOW(disp)
    hbm = pl.BlockSpec(memory_space=pl.ANY)
    copies = 19
    return pl.pallas_call(
        functools.partial(fixed, ncol, nrow),
        out_shape=pltpu.VMEM((rows, width, outs), BF16),
        in_specs=[hbm] * 4,
        out_specs=pl.BlockSpec(memory_space=pltpu.VMEM),
        scratch_shapes=[
            pltpu.VMEM((rows + 4, span, chans), BF16),
            pltpu.VMEM((rows + 4, vol_cols(width), chans), BF16),
            pltpu.VMEM((rows + 4, span, chans), BF16),
            pltpu.VMEM((rows + 4, vol_cols(width) + G, 3 * disp), BF16),
            pltpu.VMEM((rows + 2, width + 3 * G, 3 * outs), BF16),
            pltpu.VMEM(w1.shape, BF16),
            pltpu.VMEM(w2.shape, BF16),
            pltpu.SemaphoreType.DMA((4,)),
            pltpu.SemaphoreType.DMA((copies,)),
            pltpu.SemaphoreType.DMA((copies,)),
        ],
        compiler_params=pltpu.CompilerParams(
            collective_id=0, has_side_effects=True,
            vmem_limit_bytes=67_043_328 - 2 * rows * width * outs - 2**18
        ),
    )(left, right, w1, w2)


def fixed(ncol, nrow, *refs):
    kernel(ncol, nrow, *refs)


def solution(mesh):
    in_specs = (P(("strip", "row"), "col", None), P(("strip", "row"), "col", None), P(), P())
    out_specs = P(("strip", "row"), "col", None)
    return jax.shard_map(
        functools.partial(local, mesh.shape["col"], mesh.shape["row"]),
        mesh=mesh, in_specs=in_specs, out_specs=out_specs, check_vma=False,
    )
```
